32 devices in a mesh: band: 4 (over y, core), ga: 8 (over z, x).
Axes of the slice: x: 2, y: 2, z: 4, core: 2. Of those that a mesh axis runs over, the one named last changes fastest.
Arguments:
- density: float32 [160, 160, 160], P('ga'), may hold values from -6 to 6
- stick_column: int32 [20480], replicated, may hold values from 0 to 25599, as said below
- vloc: float32 [2, 160, 20480], P(None, None, 'ga'), may hold values from -0.0034179688 to 0.0034179688
- positions: float32 [3, 32], replicated, may hold values from 0 to 1
- species: int32 [32], replicated, may hold values from 0 to 1
- psi: bfloat16 [270336, 2, 1024], P('ga', None, 'band'), may hold values from -6 to 6
- miller_wave: int32 [3, 270336], P(None, 'ga'), may hold values from -40 to 40
- proj_radial: float32 [2, 8, 270336], P(None, None, 'ga'), may hold values from -0.01171875 to 0.01171875
- proj_count: int32 [2], replicated, may hold values from 4 to 8
- dcoef: float32 [2, 8, 8], replicated, may hold values from -0.0625 to 0.0625
- occupation: float32 [1024], P('band'), may hold values from 0 to 2
Outputs:
- density_sticks: float32 [2, 160, 20480], P(None, None, 'ga')
- forces: float32 [3, 32], replicated
The draws below stay inside these ranges and needn't reach their ends.
Inputs may be any that keep to these rules, and one draw needn't show every extreme that they name: `stick_column`: distinct columns of the 160 by 160 frequency plane.
All inputs are finite; a program needn't handle non-finite values.
Results may differ from the reference program's by a relative error of at most 0.0036.
Values sent between devices are 32-bit elements; how exact they have to be, the bound alone decides.
A program may use at most 192 MiB of HBM per device.

```python
import math
import jax
import jax.numpy as jnp
from jax import lax

NX = 160
NY = 160
NZ = 160
NSTICK = 20480
NPW = 270336
BANDS = 1024
NSP = 2
PSLOT = 8
ATOMS = 32


def draw_stick_column(key, part):
    return jax.random.permutation(key, NX * NY)[:NSTICK].astype(jnp.int32)


def touch_ends(drawn, rng, low, largest):
    dims = drawn.shape
    index_at = [jax.random.randint(jax.random.fold_in(rng, axis), (), 0, dims[axis]) for axis in range(len(dims))]
    drawn = drawn.at[tuple(index_at)].set(low)
    longest = dims.index(max(dims))
    index_at[longest] = (index_at[longest] + 1) % dims[longest]
    return drawn.at[tuple(index_at)].set(largest)


def levels(rng, extent, cuts, smallest, largest):
    def one(axis_at, blocks):
        heights = jax.random.uniform(jax.random.fold_in(jax.random.fold_in(rng, 6), axis_at), (blocks,), jnp.float32, smallest / len(cuts), largest / len(cuts))
        return jnp.repeat(jnp.exp(heights), extent[axis_at] // blocks).reshape((-1,) + (1,) * (len(extent) - axis_at - 1))

    factor_of = one(*cuts[0])
    for cut in cuts[1:]:
        factor_of = factor_of * one(*cut)
    return factor_of


def gaussian(stream_key, shape, deviation, reach, cuts=(), kind=jnp.bfloat16):
    array = deviation * jax.random.normal(stream_key, shape, jnp.float32)
    if cuts:
        array = array * levels(stream_key, shape, cuts, -0.22, 0.18)
    return jnp.clip(array, -reach, reach).astype(kind)


def setup_inputs(seed: int = 0) -> dict:
    streams_of = jax.random.split(jax.random.key(seed), 12)
    density = gaussian(streams_of[0], (NZ, NX, NY), 1.0, 6.0, ((0, 8),), jnp.float32)
    stick_column = draw_stick_column(jax.random.fold_in(streams_of[11], 71), 0)
    vloc = gaussian(streams_of[2], (NSP, NZ, NSTICK), (NZ * NSTICK) ** -0.5, 0.0034179688, ((2, 8),), jnp.float32)
    positions = jnp.clip(jax.random.uniform(streams_of[3], (3, ATOMS), jnp.float32, 0.0, 1.0), 0.0, 1.0)
    species = touch_ends(jax.random.randint(streams_of[4], (ATOMS,), 0, NSP), jax.random.fold_in(streams_of[4], 1), 0, NSP - 1).astype(jnp.int32)
    psi = gaussian(streams_of[5], (NPW, 2, BANDS), 1.0, 6.0, ((0, 8), (2, 4)))
    miller_wave = touch_ends(jax.random.randint(streams_of[6], (3, NPW), 0 - NX // 4, NX // 4 + 1), jax.random.fold_in(streams_of[6], 1), 0 - NX // 4, (NX // 4 + 1) - 1).astype(jnp.int32)
    proj_radial = gaussian(streams_of[7], (NSP, PSLOT, NPW), NPW ** -0.5, 0.01171875, ((2, 8),), jnp.float32)
    proj_count = jax.random.randint(streams_of[8], (NSP,), 4, PSLOT + 1).astype(jnp.int32)
    dcoef = gaussian(streams_of[9], (NSP, PSLOT, PSLOT), 0.004, 0.0625, (), jnp.float32)
    occupation = jnp.clip(2.0 * jax.random.uniform(streams_of[10], (BANDS,), jnp.float32) ** levels(streams_of[10], (BANDS,), ((0, 4),), -0.2, 0.2), 0.0, 2.0)
    return dict(density=density, stick_column=stick_column, vloc=vloc, positions=positions, species=species, psi=psi, miller_wave=miller_wave, proj_radial=proj_radial, proj_count=proj_count, dcoef=dcoef, occupation=occupation)


TWO_PI = 2.0 * math.pi
EXACT = lax.Precision.HIGHEST

def frequency(index, count):
    return jnp.where(index >= count // 2, index - count, index)

def reference(density, stick_column, vloc, positions, species, psi, miller_wave, proj_radial, proj_count, dcoef, occupation):
    spectrum = jnp.fft.fftn(density) * (1.0 / math.sqrt(NX * NY * NZ))
    picked = spectrum.reshape(NZ, NX * NY)[:, stick_column]
    stick_re = jnp.real(picked)
    stick_im = jnp.imag(picked)
    density_sticks = jnp.stack([stick_re, stick_im])
    freq_x = frequency(stick_column // NY, NX).astype(jnp.float32)
    freq_y = frequency(stick_column % NY, NY).astype(jnp.float32)
    freq_z = frequency(jnp.arange(NZ, dtype=jnp.int32), NZ).astype(jnp.float32)
    wave_x = TWO_PI / NX * freq_x
    wave_y = TWO_PI / NY * freq_y
    wave_z = TWO_PI / NZ * freq_z

    def local_atom(atom):
        place = positions[:, atom]
        angle = TWO_PI * (freq_z[:, None] * place[2] + (freq_x * place[0] + freq_y * place[1])[None, :])
        weight = vloc[species[atom]] * (stick_re * jnp.sin(angle) + stick_im * jnp.cos(angle))
        return jnp.stack([jnp.sum(weight * wave_x[None, :]), jnp.sum(weight * wave_y[None, :]), jnp.sum(weight * wave_z[:, None])])
    local_force = lax.map(local_atom, jnp.arange(ATOMS, dtype=jnp.int32)).T
    miller_f = miller_wave.astype(jnp.float32)
    weights = jnp.stack([jnp.ones_like(miller_f[0]), TWO_PI / NX * miller_f[0], TWO_PI / NY * miller_f[1], TWO_PI / NZ * miller_f[2]])
    psi_flat = psi.reshape(NPW, 2 * BANDS)
    live_slots = (jnp.arange(PSLOT, dtype=jnp.int32)[None, :] < proj_count[:, None]).astype(jnp.float32)

    def nonlocal_atom(atom):
        place = positions[:, atom]
        kind = species[atom]
        phase = TWO_PI * (place[0] * miller_f[0] + place[1] * miller_f[1] + place[2] * miller_f[2])
        radial = proj_radial[kind]
        parts = jnp.stack([radial * jnp.cos(phase)[None, :], radial * jnp.sin(phase)[None, :]], axis=1)
        table = (parts[:, None] * weights[None, :, None, :]).astype(jnp.bfloat16)
        product = jnp.dot(table.reshape(PSLOT * 8, NPW), psi_flat, preferred_element_type=jnp.float32)
        product = product.reshape(PSLOT, 4, 2, 2, BANDS)
        proj_re = product[:, :, 0, 0] - product[:, :, 1, 1]
        proj_im = product[:, :, 0, 1] + product[:, :, 1, 0]
        live = live_slots[kind]
        coupling = dcoef[kind] * live[:, None] * live[None, :]
        mixed_re = jnp.einsum('ij,jcn->icn', coupling, proj_re[:, 1:], precision=EXACT)
        mixed_im = jnp.einsum('ij,jcn->icn', coupling, proj_im[:, 1:], precision=EXACT)
        value = proj_re[:, 0][:, None, :] * mixed_im - proj_im[:, 0][:, None, :] * mixed_re
        return 2.0 * jnp.einsum('icn,n->c', value, occupation, precision=EXACT)
    nonlocal_force = lax.map(nonlocal_atom, jnp.arange(ATOMS, dtype=jnp.int32)).T
    forces = local_force + nonlocal_force
    return (density_sticks, forces)
```

```python
import math

import jax
import jax.numpy as jnp
from jax import lax
from jax.sharding import PartitionSpec as P

NX = 160
NY = 160
NZ = 160


TWO_PI = 2.0 * math.pi
EXACT = lax.Precision.HIGHEST
FINE = lax.Precision.HIGH


def frequency(index, count):
    return jnp.where(index >= count // 2, index - count, index)


def dft_table(count):
    index = jnp.arange(count, dtype=jnp.int32)
    angle = TWO_PI / count * (index[:, None] * index[None, :] % count).astype(jnp.float32)
    return (jnp.cos(angle), jnp.sin(angle))


def shards(
    density,
    stick_column,
    vloc,
    positions,
    species,
    psi,
    miller_wave,
    proj_radial,
    proj_count,
    dcoef,
    occupation,
):
    ga_index = lax.axis_index("ga")
    band_index = lax.axis_index("band")
    ga_count = lax.axis_size("ga")
    band_count = lax.axis_size("band")
    atom_count = positions.shape[1]
    kind_count = vloc.shape[0]
    slot_count = proj_radial.shape[1]
    sticks_here = vloc.shape[2]
    planes = density.shape[0]
    scale_norm = 1.0 / math.sqrt(NX * NY * NZ)
    start_zero = jnp.int32(0)
    cos_y, sin_y = dft_table(NY)
    cos_x, sin_x = dft_table(NX)
    batch_cos = jnp.broadcast_to(cos_x[None], (planes, NX, NX))
    batch_sin = jnp.broadcast_to(sin_x[None], (planes, NX, NX))
    xpass_real = jnp.einsum("pmx,pxy->pmy", batch_cos, density, precision=FINE).reshape(
        planes * NX, NY
    )
    xpass_imag = -jnp.einsum("pmx,pxy->pmy", batch_sin, density, precision=FINE).reshape(
        planes * NX, NY
    )
    full_real = jnp.dot(xpass_real, cos_y, precision=FINE) + jnp.dot(
        xpass_imag, sin_y, precision=FINE
    )
    full_imag = jnp.dot(xpass_imag, cos_y, precision=FINE) - jnp.dot(
        xpass_real, sin_y, precision=FINE
    )
    columns = jnp.concatenate(
        [full_real.reshape(planes, NX * NY), full_imag.reshape(planes, NX * NY)], axis=0
    )
    sub_sticks = sticks_here // band_count
    share_columns = lax.dynamic_slice_in_dim(
        stick_column.reshape(ga_count, band_count, sub_sticks), band_index, 1, 1
    ).reshape(ga_count * sub_sticks)
    picked_rows = jnp.take(columns.T, share_columns, axis=0)
    chosen = picked_rows.T.reshape(2 * planes, ga_count, sub_sticks).transpose(1, 0, 2)
    by_stick = lax.all_to_all(chosen, "ga", split_axis=0, concat_axis=0, tiled=True)
    by_stick = by_stick.reshape(ga_count * 2 * planes, sub_sticks)
    cos_z, sin_z = dft_table(NZ)
    cos_z = cos_z.reshape(NZ, ga_count, planes) * scale_norm
    sin_z = sin_z.reshape(NZ, ga_count, planes) * scale_norm
    table_z = jnp.stack(
        [jnp.stack([cos_z, sin_z], axis=2), jnp.stack([-sin_z, cos_z], axis=2)]
    ).reshape(2 * NZ, ga_count * 2 * planes)
    sub_values = jnp.dot(table_z, by_stick, precision=FINE).reshape(2, NZ, sub_sticks)
    density_sticks = lax.all_gather(sub_values, "band", axis=2, tiled=True)
    stick_start = ga_index * sticks_here + band_index * sub_sticks
    owned = lax.dynamic_slice_in_dim(stick_column, stick_start, sub_sticks)
    freq_x = frequency(owned // NY, NX).astype(jnp.float32)
    freq_y = frequency(owned % NY, NY).astype(jnp.float32)
    freq_z = frequency(jnp.arange(NZ, dtype=jnp.int32), NZ).astype(jnp.float32)
    wave_x = TWO_PI / NX * freq_x
    wave_y = TWO_PI / NY * freq_y
    wave_z = TWO_PI / NZ * freq_z
    angle_plane = TWO_PI * (
        positions[0][:, None] * freq_x[None, :] + positions[1][:, None] * freq_y[None, :]
    )
    angle_depth = TWO_PI * positions[2][:, None] * freq_z[None, :]
    plane_cos = jnp.cos(angle_plane)
    plane_sin = jnp.sin(angle_plane)
    plane_rows = jnp.stack(
        [
            plane_cos * wave_x[None, :],
            plane_cos * wave_y[None, :],
            plane_cos,
            plane_sin * wave_x[None, :],
            plane_sin * wave_y[None, :],
            plane_sin,
        ]
    ).reshape(6 * atom_count, sub_sticks)
    vloc_here = lax.dynamic_slice_in_dim(vloc, band_index * sub_sticks, sub_sticks, 2)
    fields = (vloc_here[:, None] * sub_values[None]).reshape(kind_count * 2 * NZ, sub_sticks)
    sums = lax.dot_general(plane_rows, fields, (((1,), (1,)), ((), ())), precision=FINE)
    sums = sums.reshape(2, 3, atom_count, kind_count, 2, NZ)
    all_pick = (species[:, None] == jnp.arange(kind_count, dtype=jnp.int32)[None, :]).astype(
        jnp.float32
    )
    sums = jnp.sum(sums * all_pick[None, None, :, :, None, None], axis=3)
    summed_real = sums[0, :, :, 0] - sums[1, :, :, 1]
    summed_imag = sums[0, :, :, 1] + sums[1, :, :, 0]
    depth_weight = jnp.stack([jnp.ones_like(wave_z), jnp.ones_like(wave_z), wave_z])
    local_part = jnp.sum(
        (
            jnp.cos(angle_depth)[None] * summed_imag + jnp.sin(angle_depth)[None] * summed_real
        )
        * depth_weight[:, None, :],
        axis=2,
    )
    bands_here = psi.shape[2]
    waves_here = psi.shape[0]
    psi_flat = psi.reshape(waves_here, 2 * bands_here)
    miller_f = miller_wave.astype(jnp.float32)
    weights = jnp.stack(
        [
            jnp.ones_like(miller_f[0]),
            TWO_PI / NX * miller_f[0],
            TWO_PI / NY * miller_f[1],
            TWO_PI / NZ * miller_f[2],
        ]
    )

    def project_block(block_start, block_rows):
        block_atoms = block_rows // slot_count
        atom_start = block_start // slot_count
        block_places = lax.dynamic_slice_in_dim(positions, atom_start, block_atoms, 1)
        block_kinds = lax.dynamic_slice_in_dim(species, atom_start, block_atoms)
        phase = TWO_PI * (
            block_places[0][:, None] * miller_f[0][None, :]
            + block_places[1][:, None] * miller_f[1][None, :]
            + block_places[2][:, None] * miller_f[2][None, :]
        )
        radial = jnp.zeros((block_atoms, slot_count, waves_here), jnp.float32)
        for kind_index in range(kind_count):
            match = (block_kinds == kind_index).astype(jnp.float32)
            radial = radial + match[:, None, None] * proj_radial[kind_index][None]
        parts = jnp.stack(
            [radial * jnp.cos(phase)[:, None, :], radial * jnp.sin(phase)[:, None, :]], axis=2
        )
        table = (parts[:, :, None] * weights[None, None, :, None, :]).astype(jnp.bfloat16)
        product = jnp.dot(
            table.reshape(block_rows * 8, waves_here), psi_flat, preferred_element_type=jnp.float32
        )
        product = product.reshape(block_rows, 4, 2, 2, bands_here)
        proj_real = product[:, :, 0, 0] - product[:, :, 1, 1]
        proj_imag = product[:, :, 0, 1] + product[:, :, 1, 0]
        return jnp.stack([proj_real, proj_imag], axis=2).reshape(block_rows, 8 * bands_here)

    share_rows = atom_count * slot_count // ga_count
    block_rows = 64
    starts = block_rows * jnp.arange(
        share_rows * lax.axis_size("ga") // block_rows, dtype=jnp.int32
    )

    def one_block(block_start):
        return project_block(block_start, block_rows)

    owned_rows = lax.psum_scatter(
        lax.map(one_block, starts).reshape(share_rows * lax.axis_size("ga"), 8 * bands_here),
        "ga",
        scatter_dimension=0,
        tiled=True,
    )
    per_ga = share_rows // slot_count
    ga_start = ga_index * per_ga
    terms = owned_rows.reshape(per_ga, slot_count, 4, 2, bands_here)
    ga_kinds = lax.dynamic_slice_in_dim(species, ga_start, per_ga)
    ga_pick = (ga_kinds[:, None] == jnp.arange(kind_count, dtype=jnp.int32)[None, :]).astype(
        jnp.float32
    )
    live_slots = (jnp.arange(slot_count, dtype=jnp.int32)[None, :] < proj_count[:, None]).astype(
        jnp.float32
    )
    kind_table = dcoef * live_slots[:, :, None] * live_slots[:, None, :]
    coupling = jnp.einsum("as,sij->aij", ga_pick, kind_table, precision=EXACT)
    mixed_real = jnp.einsum("aij,ajcn->aicn", coupling, terms[:, :, 1:, 0], precision=EXACT)
    mixed_imag = jnp.einsum("aij,ajcn->aicn", coupling, terms[:, :, 1:, 1], precision=EXACT)
    value = (
        terms[:, :, 0, 0][:, :, None, :] * mixed_imag
        - terms[:, :, 0, 1][:, :, None, :] * mixed_real
    )
    nonlocal_part = 2.0 * jnp.einsum("aicn,n->ca", value, occupation, precision=EXACT)
    nonlocal_full = lax.dynamic_update_slice(
        jnp.zeros((3, atom_count), jnp.float32), nonlocal_part, (start_zero, ga_start)
    )
    forces = lax.psum(local_part + nonlocal_full, ("band", "ga"))
    return (density_sticks, forces)


def solution(mesh):
    in_specs = (
        P("ga", None, None),
        P(),
        P(None, None, "ga"),
        P(),
        P(),
        P("ga", None, "band"),
        P(None, "ga"),
        P(None, None, "ga"),
        P(),
        P(),
        P("band"),
    )
    out_specs = (P(None, None, "ga"), P())
    return jax.shard_map(shards, mesh=mesh, in_specs=in_specs, out_specs=out_specs, check_vma=False)
```
